32 devices in a mesh: gz: 8 (over z, y), gy: 4 (over x, core).
Axes of the slice: x: 2, y: 2, z: 4, core: 2. Of those that a mesh axis runs over, the one named last changes fastest.
Arguments:
- phase: float32 [32, 128, 768], P('gz', 'gy'), may hold values from 0 to 1
- solute: float32 [32, 128, 768], P('gz', 'gy'), may hold values from -0.5 to 0.5
- labels: int32 [32, 128, 768], P('gz', 'gy'), may hold values from 0 to 31
- quat_table: float32 [32, 4], replicated, may hold values from -3 to 3
- heat_map: float32 [128, 768], P('gy'), may hold values from -4 to 4
- cotangent: float32 [6, 32, 128, 768], P(None, 'gz', 'gy'), may hold values from -6 to 6
Outputs:
- final_fields: float32 [6, 32, 128, 768], P(None, 'gz', 'gy')
- sensitivity: float32 [128, 768], P('gy')
- objective: float32 [], replicated
The draws below stay inside these ranges and needn't reach their ends.
All inputs are finite; a program needn't handle non-finite values.
Results may differ from the reference program's by a relative error of at most 0.0003.
Values sent between devices are 32-bit elements; how exact they have to be, the bound alone decides.
A program may use at most 128 MiB of HBM per device.

```python
import jax
import jax.numpy as jnp
from jax import lax

NX = 768
GRAINS = 32
NY = 128
NZ = 32


def touch_ends(drawn, key, least, high):
    longest = drawn.shape.index(max(drawn.shape))
    spots = []
    for shift in (0, 1):
        where = [jax.random.randint(jax.random.fold_in(key, axis), (), 0, length) for axis, length in enumerate(drawn.shape)]
        where[longest] = (where[longest] + shift) % drawn.shape[longest]
        spots.append(tuple(where))
    return drawn.at[spots[0]].set(least).at[spots[1]].set(high)


def block_levels(rng, shape, split, least, high):
    def one(position, blocks):
        heights = jax.random.uniform(jax.random.fold_in(jax.random.fold_in(rng, 6), position), (blocks,), jnp.float32, least / len(split), high / len(split))
        return jnp.repeat(jnp.exp(heights), shape[position] // blocks).reshape((-1,) + (1,) * (len(shape) - position - 1))

    loudness = one(*split[0])
    for cut in split[1:]:
        loudness = loudness * one(*cut)
    return loudness


def normal_values(own_key, extent, spread, reach, pieces=(), kind=jnp.bfloat16):
    array = spread * jax.random.normal(own_key, extent, jnp.float32)
    if pieces:
        array = array * block_levels(own_key, extent, pieces, -0.22, 0.18)
    return jnp.clip(array, -reach, reach).astype(kind)


def setup_inputs(seed: int = 0) -> dict:
    streams_of = jax.random.split(jax.random.key(seed), 7)
    phase = jnp.clip(1.0 * jax.random.uniform(streams_of[0], (NZ, NY, NX), jnp.float32) ** block_levels(streams_of[0], (NZ, NY, NX), ((0, 8), (1, 4)), -0.2, 0.2), 0.0, 1.0)
    solute = jnp.clip(jax.random.uniform(streams_of[1], (NZ, NY, NX), jnp.float32, -0.5, 0.5) * block_levels(streams_of[1], (NZ, NY, NX), ((0, 8), (1, 4)), -0.4, 0.0), -0.5, 0.5)
    labels = touch_ends(jax.random.randint(streams_of[2], (NZ, NY, NX), 0, GRAINS), jax.random.fold_in(streams_of[2], 1), 0, GRAINS - 1).astype(jnp.int32)
    quat_table = normal_values(streams_of[3], (GRAINS, 4), 0.5, 3.0, (), jnp.float32)
    heat_map = normal_values(streams_of[4], (NY, NX), 1.0, 4.0, ((0, 4),), jnp.float32)
    cotangent = normal_values(streams_of[5], (6, NZ, NY, NX), 1.0, 6.0, ((1, 8), (2, 4)), jnp.float32)
    return {"phase": phase, "solute": solute, "labels": labels, "quat_table": quat_table, "heat_map": heat_map, "cotangent": cotangent}


time_step = 0.08
drive_gain = 0.6
misfit_gain = 0.2
solute_diff = 0.8
reject_gain = 0.5
solute_shift = 0.5

def advance(padded, heat_rows):
    center = padded[:, 1:-1, 1:-1, :]
    border = jnp.zeros_like(center[..., :1])
    laplace = padded[:, 2:, 1:-1, :] + padded[:, :-2, 1:-1, :] + padded[:, 1:-1, 2:, :] + padded[:, 1:-1, :-2, :] + jnp.concatenate([center[..., 1:], border], -1) + jnp.concatenate([border, center[..., :-1]], -1) - 6.0 * center
    phase_now = center[0]
    quaternions = center[1:5]
    solute_now = center[5]
    undercool = heat_rows[None] - solute_shift * solute_now
    misfit = lax.optimization_barrier(jnp.sum(quaternions * laplace[1:5], axis=0))
    phase_next = phase_now + time_step * (laplace[0] + 4.0 * phase_now * (1.0 - phase_now) * (phase_now - 0.5 + drive_gain * jnp.tanh(undercool)) + misfit_gain * phase_now * misfit)
    quat_next = quaternions + time_step * ((1.0 - phase_now) ** 2 + 0.1) * laplace[1:5]
    solute_next = solute_now + time_step * solute_diff * laplace[5] + reject_gain * (phase_next - phase_now) * solute_now
    return jnp.concatenate([phase_next[None], quat_next, solute_next[None]], 0)

def surround(fields):
    wrapped = jnp.concatenate([fields[:, -1:], fields, fields[:, :1]], 1)
    return jnp.pad(wrapped, ((0, 0), (0, 0), (1, 1), (0, 0)))

def reference(phase, solute, labels, quat_table, heat_map, cotangent):
    quaternions = jnp.moveaxis(quat_table[labels], -1, 0)
    initial = jnp.concatenate([phase[None], quaternions, solute[None]], 0)

    def forward(heat):
        return advance(surround(advance(surround(initial), heat)), heat)
    final_fields, pullback = jax.vjp(forward, heat_map)
    sensitivity = pullback(cotangent)[0]
    objective = jnp.sum(cotangent * final_fields)
    return (final_fields, sensitivity, objective)
```

```python
import functools

import jax
import jax.numpy as jnp
from jax import lax
from jax.experimental import pallas as pl
from jax.experimental.pallas import tpu as pltpu
from jax.sharding import PartitionSpec as P

MESH = pl.DeviceIdType.MESH
F32 = jnp.float32


def kernel(
    n, m, depth, rows, cols, per,
    phase, solute, labels, table, heat, cot,
    out, sens_out, obj_out,
    E, lab, M, G, GP, CQ, W0, sbuf, rbuf, obuf, orbuf, red, fin,
    lsem, ysend, yrecv, zsend, zrecv, csend, crecv, r1s, r1r, os, orr, r2s, r2r,
):
    gz = lax.axis_index("gz")
    gy = lax.axis_index("gy")
    up = lax.rem(gz + 1, n)
    down = lax.rem(gz + n - 1, n)
    is_low = gy == 0
    is_high = gy == m - 1
    low = jnp.maximum(gy - 1, 0)
    high = jnp.minimum(gy + 1, m - 1)
    tiles = rows // 8
    lanes = cols // 128
    D = depth
    own = pl.ds(8, rows)
    top = 8 + rows

    bar = pltpu.get_barrier_semaphore()
    for d in range(1, n):
        pl.semaphore_signal(bar, inc=1, device_id=(lax.rem(gz + d, n), gy), device_id_type=MESH)
    for d in range(1, m):
        pl.semaphore_signal(bar, inc=1, device_id=(gz, lax.rem(gy + d, m)), device_id_type=MESH)

    local = []
    dests = ((phase, E.at[0]), (solute, E.at[5]), (labels, lab))
    for k, (src, dst) in enumerate(dests):
        local.append(pltpu.make_async_copy(src, dst.at[pl.ds(2, D), own], lsem.at[k]))
    local.append(pltpu.make_async_copy(cot.at[0], G.at[0, pl.ds(1, D), own], lsem.at[3]))
    local.append(pltpu.make_async_copy(cot.at[5], G.at[1, pl.ds(1, D), own], lsem.at[4]))
    local.append(pltpu.make_async_copy(cot.at[pl.ds(1, 4)], CQ, lsem.at[5]))
    for copy in local:
        copy.start()

    pl.semaphore_wait(bar, n - 1 + m - 1)

    def remote(src, dst, ss, rs, z, y):
        return pltpu.make_async_remote_copy(
            src_ref=src, dst_ref=dst, send_sem=ss, recv_sem=rs, device_id=(z, y), device_id_type=MESH
        )

    zc = {1: [], 2: []}
    i = 0
    for width in (1, 2):
        for src, dst in dests:
            zc[width].append(remote(src.at[D - width], dst.at[2 - width, own], zsend.at[i], zrecv.at[i], up, gy))
            zc[width].append(
                remote(src.at[width - 1], dst.at[D + 1 + width, own], zsend.at[i + 1], zrecv.at[i + 1], down, gy)
            )
            i += 2
    for copy in zc[1]:
        copy.start()
    to_high, to_low = [], []
    faces = [(s, d.at[pl.ds(2, D)]) for s, d in dests]
    faces += [(cot.at[0], G.at[0, pl.ds(1, D)]), (cot.at[5], G.at[1, pl.ds(1, D)])]
    for k, (src, dst) in enumerate(faces):
        to_high.append(
            remote(src.at[:, pl.ds(rows - 8, 8)], dst.at[:, pl.ds(0, 8)], ysend.at[k], yrecv.at[k], gz, high)
        )
        to_low.append(
            remote(src.at[:, pl.ds(0, 8)], dst.at[:, pl.ds(top, 8)], ysend.at[5 + k], yrecv.at[5 + k], gz, low)
        )

    @pl.when(jnp.logical_not(is_high))
    def _():
        for copy in to_high:
            copy.start()

    @pl.when(jnp.logical_not(is_low))
    def _():
        for copy in to_low:
            copy.start()

    for copy in zc[2]:
        copy.start()

    row = lax.broadcasted_iota(jnp.int32, (8, 128), 0)
    lane = lax.broadcasted_iota(jnp.int32, (8, 128), 1)
    zero = jnp.zeros((8, 128), F32)

    sbuf[...] = jnp.zeros_like(sbuf)
    obuf[...] = jnp.zeros_like(obuf)
    for z in (0, D + 1):
        G[1, z] = jnp.zeros((rows + 16, cols), F32)
        GP[z] = jnp.zeros((rows + 16, cols), F32)

    def ds8(t):
        return pl.ds(pl.multiple_of(t * 8, 8), 8)

    def expand(z, t):
        r = ds8(t)
        for j in range(lanes):
            x = pl.ds(j * 128, 128)
            ids = lab[z, r, x]
            for k in range(4):
                E[1 + k, z, r, x] = jnp.take_along_axis(table[k], ids, axis=1)

    def wipe(z, t):
        r = ds8(t)
        for k in range(6):
            E[k, z, r, :] = jnp.zeros((8, cols), F32)

    def loop(count, body):
        def step(i, carry):
            body(i)
            return carry

        lax.fori_loop(0, count, step, 0)

    def around(ref, lead, z, t, j, last):
        r, x = ds8(t), pl.ds(j * 128, 128)
        c = ref[(*lead, z, r, x)]
        before = ref[(*lead, z, ds8(jnp.maximum(t - 1, 0)), x)]
        after = ref[(*lead, z, ds8(jnp.minimum(t + 1, last)), x)]
        left = ref[(*lead, z, r, pl.ds((j - 1) * 128, 128))] if j else zero
        right = ref[(*lead, z, r, pl.ds((j + 1) * 128, 128))] if j < lanes - 1 else zero
        ys = pltpu.roll(jnp.where(row == 0, after, c), 7, 0) + pltpu.roll(jnp.where(row == 7, before, c), 1, 0)
        xs = pltpu.roll(jnp.where(lane == 0, right, c), 127, 1) + pltpu.roll(jnp.where(lane == 127, left, c), 1, 1)
        zs = ref[(*lead, z + 1, r, x)] + ref[(*lead, z - 1, r, x)]
        return c, zs + ys + xs - 6.0 * c

    def mid(z, t, inside):
        r = ds8(t)
        drop = ((t == 0) & is_low) | ((t == tiles + 1) & is_high)
        keep = jnp.where(drop, 0.0, 1.0)
        hr = ds8(t)
        for j in range(lanes):
            x = pl.ds(j * 128, 128)
            p, lp = around(E, (0,), z, t, j, tiles + 1)
            c, lc = around(E, (5,), z, t, j, tiles + 1)
            misfit = zero
            rate = 0.08 * ((1.0 - p) * (1.0 - p) + 0.1)
            for k in range(4):
                q, lq = around(E, (1 + k,), z, t, j, tiles + 1)
                misfit = misfit + q * lq
                M[1 + k, z - 1, r, x] = keep * (q + rate * lq)
            th = jnp.tanh(heat[hr, x] - 0.5 * c)
            pq = p * (1.0 - p)
            dp = 0.08 * (lp + 4.0 * pq * (p - 0.5 + 0.6 * th) + 0.2 * p * misfit)
            cn = keep * (c + 0.064 * lc + 0.5 * dp * c)
            M[0, z - 1, r, x] = keep * (p + dp)
            M[5, z - 1, r, x] = cn
            W0[z - 1, r, x] = 0.192 * pq * (1.0 - th * th)
            if inside:
                GP[z - 1, r, x] = G[0, z - 1, r, x] + 0.5 * cn * G[1, z - 1, r, x]

    def final(z, t, edge):
        zm = z - 1
        r = ds8(t)
        ro = ds8(t - 1)
        for j in range(lanes):
            x = pl.ds(j * 128, 128)
            p, lp = around(M, (0,), zm, t, j, tiles + 1)
            c, lc = around(M, (5,), zm, t, j, tiles + 1)
            gc, lgc = around(G, (1,), zm, t, j, tiles + 1)
            gp, lgp = around(GP, (), zm, t, j, tiles + 1)
            g0 = G[0, zm, r, x]
            rate = 0.08 * ((1.0 - p) * (1.0 - p) + 0.1)
            misfit, qterm, obj = zero, zero, zero
            for k in range(4):
                q, lq = around(M, (1 + k,), zm, t, j, tiles + 1)
                g = CQ[k, z - 2, ro, x]
                qn = q + rate * lq
                out[1 + k, z - 2, ro, x] = qn
                misfit = misfit + q * lq
                qterm = qterm + g * lq
                obj = obj + g * qn
            th = jnp.tanh(heat[r, x] - 0.5 * c)
            pq = p * (1.0 - p)
            drive = p - 0.5 + 0.6 * th
            dp = 0.08 * (lp + 4.0 * pq * drive + 0.2 * p * misfit)
            pn = p + dp
            cn = c + 0.064 * lc + 0.5 * dp * c
            out[0, z - 2, ro, x] = pn
            out[5, z - 2, ro, x] = cn
            obuf[...] += obj + g0 * pn + gc * cn
            w = 0.192 * pq * (1.0 - th * th)
            gw = gp * w
            lam_p = (
                gp * (1.0 + 0.08 * (4.0 * (1.0 - 2.0 * p) * drive + 4.0 * pq + 0.2 * misfit))
                + 0.08 * lgp
                - 0.5 * c * gc
                - 0.16 * (1.0 - p) * qterm
            )
            lam_c = gc * (1.0 + 0.5 * dp) + 0.064 * lgc - 0.5 * gw
            s = gw + (lam_p + 0.5 * E[5, z, r, x] * lam_c) * W0[zm, r, x]
            if edge is not None:
                s = s + W0[edge - 1, r, x] * (0.08 * gp + 0.032 * E[5, edge, r, x] * gc)
            b = (t - 1) * lanes + j
            sbuf[b] += s

    def grid(z0, zstep, t0, count, body):
        loop(2 * count, lambda i: body(z0 + zstep * (i // count), t0 + i % count))

    for copy in local[:3]:
        copy.wait()
    loop(D * tiles, lambda i: expand(2 + i // tiles, 1 + i % tiles))

    @pl.when(jnp.logical_not(is_low))
    def _():
        for copy in to_high:
            copy.wait_recv()
        loop(D, lambda i: expand(2 + i, 0))

    @pl.when(is_low)
    def _():
        loop(D + 2, lambda i: wipe(1 + i, 0))
        for k in range(2):
            for z in range(D):
                G[k, 1 + z, pl.ds(0, 8), :] = jnp.zeros((8, cols), F32)

    @pl.when(jnp.logical_not(is_high))
    def _():
        for copy in to_low:
            copy.wait_recv()
        loop(D, lambda i: expand(2 + i, tiles + 1))

    @pl.when(is_high)
    def _():
        loop(D + 2, lambda i: wipe(1 + i, tiles + 1))
        for k in range(2):
            for z in range(D):
                G[k, 1 + z, pl.ds(top, 8), :] = jnp.zeros((8, cols), F32)

    for copy in local[3:]:
        copy.wait()
    loop((D - 2) * (tiles + 2), lambda i: mid(3 + i // (tiles + 2), i % (tiles + 2), True))

    for copy in zc[1]:
        copy.wait_recv()
    c_high, c_low = [], []
    i = 0
    for z in (1, D + 2):
        for _, dst in dests:
            c_high.append(
                remote(dst.at[z, pl.ds(rows, 8)], dst.at[z, pl.ds(0, 8)], csend.at[i], crecv.at[i], gz, high)
            )
            c_low.append(
                remote(dst.at[z, pl.ds(8, 8)], dst.at[z, pl.ds(top, 8)], csend.at[6 + i], crecv.at[6 + i], gz, low)
            )
            i += 1

    @pl.when(jnp.logical_not(is_high))
    def _():
        for copy in c_high:
            copy.start()

    @pl.when(jnp.logical_not(is_low))
    def _():
        for copy in c_low:
            copy.start()

    grid(1, D + 1, 1, tiles, expand)

    @pl.when(jnp.logical_not(is_low))
    def _():
        for copy in c_high:
            copy.wait_recv()
        loop(2, lambda i: expand(1 + (D + 1) * i, 0))

    @pl.when(jnp.logical_not(is_high))
    def _():
        for copy in c_low:
            copy.wait_recv()
        loop(2, lambda i: expand(1 + (D + 1) * i, tiles + 1))

    grid(2, D - 1, 0, tiles + 2, lambda z, t: mid(z, t, True))
    loop((D - 2) * tiles, lambda i: final(3 + i // tiles, 1 + i % tiles, None))

    for copy in zc[2]:
        copy.wait_recv()
    grid(0, D + 3, 1, tiles, expand)
    grid(1, D + 1, 1, tiles, lambda z, t: mid(z, t, False))
    loop(2 * tiles, lambda i: final(2 + (D - 1) * (i // tiles), 1 + i % tiles, 1 + (D + 1) * (i // tiles)))

    sends = []
    for d in range(1, n):
        peer = lax.rem(gz + d, n)
        sends.append(remote(sbuf.at[pl.ds(peer * per, per)], rbuf.at[d - 1], r1s.at[d - 1], r1r.at[d - 1], peer, gy))
    for d in range(1, m):
        sends.append(remote(obuf, orbuf.at[gy], os.at[d - 1], orr.at[d - 1], gz, lax.rem(gy + d, m)))
    for copy in sends:
        copy.start()
    orbuf[gy] = obuf[...]
    for copy in sends:
        copy.wait_recv()
    acc = sbuf[pl.ds(gz * per, per)]
    for d in range(1, n):
        acc = acc + rbuf[d - 1]
    red[pl.ds(0, per)] = acc
    total = orbuf[0]
    for d in range(1, m):
        total = total + orbuf[d]
    red[per] = total
    bcast = []
    for d in range(1, n):
        bcast.append(remote(red, fin.at[gz], r2s.at[d - 1], r2r.at[d - 1], lax.rem(gz + d, n), gy))
    for copy in bcast:
        copy.start()
    fin[gz] = red[...]
    for copy in bcast:
        copy.wait_recv()
    total = fin[0, per]
    for d in range(1, n):
        total = total + fin[d, per]
    obj_out[0, 0] = jnp.sum(total)
    for b in range(tiles * lanes):
        sens_out[pl.ds(b // lanes * 8, 8), pl.ds(b % lanes * 128, 128)] = fin[b // per, b % per]

    for copy in zc[1] + zc[2] + sends + bcast:
        copy.wait_send()

    @pl.when(jnp.logical_not(is_high))
    def _():
        for copy in to_high + c_high:
            copy.wait_send()

    @pl.when(jnp.logical_not(is_low))
    def _():
        for copy in to_low + c_low:
            copy.wait_send()


def solution(mesh):
    n, m = mesh.shape["gz"], mesh.shape["gy"]

    def on_device(phase, solute, labels, quat_table, heat_map, cotangent):
        depth, rows, cols = phase.shape
        grains = quat_table.shape[0]
        blocks = rows // 8 * (cols // 128)
        per = -(-blocks // n)
        table = jnp.pad(quat_table.T, ((0, 0), (0, 128 - grains)))
        table = jnp.broadcast_to(table[:, None, :], (4, 8, 128))
        gy = lax.axis_index("gy")
        above = lax.ppermute(heat_map[-8:], "gy", [(i, i + 1) for i in range(m - 1)])
        below = lax.ppermute(heat_map[:8], "gy", [(i + 1, i) for i in range(m - 1)])
        heat = jnp.concatenate([above, heat_map, below], 0)
        tall = rows + 16
        vmem = pl.BlockSpec(memory_space=pltpu.VMEM)
        hbm = pl.BlockSpec(memory_space=pl.ANY)
        dma = lambda k: pltpu.SemaphoreType.DMA((k,))
        final, sens, obj = pl.pallas_call(
            functools.partial(kernel, n, m, depth, rows, cols, per),
            out_shape=(
                jax.ShapeDtypeStruct((6, depth, rows, cols), F32),
                jax.ShapeDtypeStruct((rows, cols), F32),
                jax.ShapeDtypeStruct((1, 1), F32),
            ),
            in_specs=[hbm, hbm, hbm, vmem, vmem, hbm],
            out_specs=(vmem, vmem, pl.BlockSpec(memory_space=pltpu.SMEM)),
            scratch_shapes=[
                pltpu.VMEM((6, depth + 4, tall, cols), F32),
                pltpu.VMEM((depth + 4, tall, cols), jnp.int32),
                pltpu.VMEM((6, depth + 2, tall, cols), F32),
                pltpu.VMEM((2, depth + 2, tall, cols), F32),
                pltpu.VMEM((depth + 2, tall, cols), F32),
                pltpu.VMEM((4, depth, rows, cols), F32),
                pltpu.VMEM((depth + 2, tall, cols), F32),
                pltpu.VMEM((n * per, 8, 128), F32),
                pltpu.VMEM((n - 1, per, 8, 128), F32),
                pltpu.VMEM((8, 128), F32),
                pltpu.VMEM((m, 8, 128), F32),
                pltpu.VMEM((per + 1, 8, 128), F32),
                pltpu.VMEM((n, per + 1, 8, 128), F32),
                dma(6), dma(10), dma(10), dma(12), dma(12), dma(12), dma(12),
                dma(n - 1), dma(n - 1), dma(m - 1), dma(m - 1), dma(n - 1), dma(n - 1),
            ],
            compiler_params=pltpu.CompilerParams(
                collective_id=0, has_side_effects=True, vmem_limit_bytes=48 * 1024 * 1024
            ),
        )(phase, solute, labels, table, heat, cotangent)
        return final, sens, obj[0, 0]

    return jax.shard_map(
        on_device,
        mesh=mesh,
        in_specs=(
            P("gz", "gy", None),
            P("gz", "gy", None),
            P("gz", "gy", None),
            P(),
            P("gy", None),
            P(None, "gz", "gy", None),
        ),
        out_specs=(P(None, "gz", "gy", None), P("gy", None), P()),
        check_vma=False,
    )
```

```python
import functools

import jax
import jax.numpy as jnp
from jax import lax
from jax.experimental import pallas as pl
from jax.experimental.pallas import tpu as pltpu
from jax.sharding import PartitionSpec as P

MESH = pl.DeviceIdType.MESH
F32 = jnp.float32


def kernel(
    n, m, depth, rows, cols, per,
    phase, solute, labels, quats, heat_in, cot,
    out, sens_out, obj_out,
    E, lab, M, G, GP, CQ, W0, heat, table, sbuf, rbuf, obuf, orbuf, red, fin,
    lsem, ysend, yrecv, zsend, zrecv, fsend, frecv, csend, crecv, r1s, r1r, os, orr, r2s, r2r,
):
    gz = lax.axis_index("gz")
    gy = lax.axis_index("gy")
    up = lax.rem(gz + 1, n)
    down = lax.rem(gz + n - 1, n)
    is_low = gy == 0
    is_high = gy == m - 1
    low = jnp.maximum(gy - 1, 0)
    high = jnp.minimum(gy + 1, m - 1)
    tiles = rows // 8
    lanes = cols // 128
    D = depth
    own = pl.ds(8, rows)
    top = 8 + rows

    bar = pltpu.get_barrier_semaphore()
    for d in range(1, n):
        pl.semaphore_signal(bar, inc=1, device_id=(lax.rem(gz + d, n), gy), device_id_type=MESH)
    for d in range(1, m):
        pl.semaphore_signal(bar, inc=1, device_id=(gz, lax.rem(gy + d, m)), device_id_type=MESH)

    local = []
    dests = ((phase, E.at[0]), (solute, E.at[5]), (labels, lab))
    for k, (src, dst) in enumerate(dests):
        local.append(pltpu.make_async_copy(src, dst.at[pl.ds(2, D), own], lsem.at[k]))
    local.append(pltpu.make_async_copy(cot.at[0], G.at[0, pl.ds(1, D), own], lsem.at[3]))
    local.append(pltpu.make_async_copy(cot.at[5], G.at[1, pl.ds(1, D), own], lsem.at[4]))
    local.append(pltpu.make_async_copy(cot.at[pl.ds(1, 4)], CQ, lsem.at[5]))
    local.append(pltpu.make_async_copy(heat_in, heat.at[own], lsem.at[6]))
    for copy in local:
        copy.start()

    pl.semaphore_wait(bar, n - 1 + m - 1)

    def remote(src, dst, ss, rs, z, y):
        return pltpu.make_async_remote_copy(
            src_ref=src, dst_ref=dst, send_sem=ss, recv_sem=rs, device_id=(z, y), device_id_type=MESH
        )

    zc = []
    for k, (src, dst) in enumerate(dests):
        zc.append(remote(src.at[D - 1], dst.at[1, own], zsend.at[2 * k], zrecv.at[2 * k], up, gy))
        zc.append(remote(src.at[0], dst.at[D + 2, own], zsend.at[2 * k + 1], zrecv.at[2 * k + 1], down, gy))

    def second(t):
        found = []
        a, b = pl.ds(pl.multiple_of(t * 8, 8), 8), pl.ds(pl.multiple_of(t * 8 + 8, 8), 8)
        for k, (src, dst) in enumerate(dests):
            found.append(remote(src.at[D - 2, a], dst.at[0, b], fsend.at[2 * k, t], frecv.at[2 * k, t], up, gy))
            found.append(
                remote(src.at[1, a], dst.at[D + 3, b], fsend.at[2 * k + 1, t], frecv.at[2 * k + 1, t], down, gy)
            )
        return found

    for copy in zc:
        copy.start()
    to_high, to_low = [], []
    faces = [(s, d.at[pl.ds(2, D)]) for s, d in dests]
    faces += [(cot.at[0], G.at[0, pl.ds(1, D)]), (cot.at[5], G.at[1, pl.ds(1, D)])]
    for k, (src, dst) in enumerate(faces):
        to_high.append(
            remote(src.at[:, pl.ds(rows - 8, 8)], dst.at[:, pl.ds(0, 8)], ysend.at[k], yrecv.at[k], gz, high)
        )
        to_low.append(
            remote(src.at[:, pl.ds(0, 8)], dst.at[:, pl.ds(top, 8)], ysend.at[6 + k], yrecv.at[6 + k], gz, low)
        )
    to_high.append(
        remote(heat_in.at[pl.ds(rows - 8, 8)], heat.at[pl.ds(0, 8)], ysend.at[5], yrecv.at[5], gz, high)
    )
    to_low.append(remote(heat_in.at[pl.ds(0, 8)], heat.at[pl.ds(top, 8)], ysend.at[11], yrecv.at[11], gz, low))

    @pl.when(jnp.logical_not(is_high))
    def _():
        for copy in to_high:
            copy.start()

    @pl.when(jnp.logical_not(is_low))
    def _():
        for copy in to_low:
            copy.start()

    for t in range(tiles):
        for copy in second(t):
            copy.start()

    row = lax.broadcasted_iota(jnp.int32, (8, 128), 0)
    lane = lax.broadcasted_iota(jnp.int32, (8, 128), 1)
    zero = jnp.zeros((8, 128), F32)

    for k in range(4):
        entry = zero
        for grain in range(quats.shape[0]):
            entry = jnp.where(lane == grain, quats[grain, k], entry)
        table[k] = entry
    sbuf[...] = jnp.zeros_like(sbuf)
    obuf[...] = jnp.zeros_like(obuf)
    for z in (0, D + 1):
        G[1, z] = jnp.zeros((rows + 16, cols), F32)
        GP[z] = jnp.zeros((rows + 16, cols), F32)

    def ds8(t):
        return pl.ds(pl.multiple_of(t * 8, 8), 8)

    def expand(z, t):
        r = ds8(t)
        for j in range(lanes):
            x = pl.ds(j * 128, 128)
            ids = lab[z, r, x]
            for k in range(4):
                E[1 + k, z, r, x] = jnp.take_along_axis(table[k], ids, axis=1)

    def wipe(z, t):
        r = ds8(t)
        for k in range(6):
            E[k, z, r, :] = jnp.zeros((8, cols), F32)

    def loop(count, body):
        def step(i, carry):
            body(i)
            return carry

        lax.fori_loop(0, count, step, 0)

    def around(ref, lead, z, t, j, last):
        r, x = ds8(t), pl.ds(j * 128, 128)
        c = ref[(*lead, z, r, x)]
        before = ref[(*lead, z, ds8(jnp.maximum(t - 1, 0)), x)]
        after = ref[(*lead, z, ds8(jnp.minimum(t + 1, last)), x)]
        left = ref[(*lead, z, r, pl.ds((j - 1) * 128, 128))] if j else zero
        right = ref[(*lead, z, r, pl.ds((j + 1) * 128, 128))] if j < lanes - 1 else zero
        ys = pltpu.roll(jnp.where(row == 0, after, c), 7, 0) + pltpu.roll(jnp.where(row == 7, before, c), 1, 0)
        xs = pltpu.roll(jnp.where(lane == 0, right, c), 127, 1) + pltpu.roll(jnp.where(lane == 127, left, c), 1, 1)
        zs = ref[(*lead, z + 1, r, x)] + ref[(*lead, z - 1, r, x)]
        return c, zs + ys + xs - 6.0 * c

    def mid(z, t, inside):
        r = ds8(t)
        drop = ((t == 0) & is_low) | ((t == tiles + 1) & is_high)
        keep = jnp.where(drop, 0.0, 1.0)
        hr = ds8(t)
        for j in range(lanes):
            x = pl.ds(j * 128, 128)
            p, lp = around(E, (0,), z, t, j, tiles + 1)
            c, lc = around(E, (5,), z, t, j, tiles + 1)
            misfit = zero
            rate = 0.08 * ((1.0 - p) * (1.0 - p) + 0.1)
            for k in range(4):
                q, lq = around(E, (1 + k,), z, t, j, tiles + 1)
                misfit = misfit + q * lq
                M[1 + k, z - 1, r, x] = keep * (q + rate * lq)
            th = jnp.tanh(heat[hr, x] - 0.5 * c)
            pq = p * (1.0 - p)
            dp = 0.08 * (lp + 4.0 * pq * (p - 0.5 + 0.6 * th) + 0.2 * p * misfit)
            cn = keep * (c + 0.064 * lc + 0.5 * dp * c)
            M[0, z - 1, r, x] = keep * (p + dp)
            M[5, z - 1, r, x] = cn
            W0[z - 1, r, x] = 0.192 * pq * (1.0 - th * th)
            if inside:
                GP[z - 1, r, x] = G[0, z - 1, r, x] + 0.5 * cn * G[1, z - 1, r, x]

    def final(z, t, edge):
        zm = z - 1
        r = ds8(t)
        ro = ds8(t - 1)
        for j in range(lanes):
            x = pl.ds(j * 128, 128)
            p, lp = around(M, (0,), zm, t, j, tiles + 1)
            c, lc = around(M, (5,), zm, t, j, tiles + 1)
            gc, lgc = around(G, (1,), zm, t, j, tiles + 1)
            gp, lgp = around(GP, (), zm, t, j, tiles + 1)
            g0 = G[0, zm, r, x]
            rate = 0.08 * ((1.0 - p) * (1.0 - p) + 0.1)
            misfit, qterm, obj = zero, zero, zero
            for k in range(4):
                q, lq = around(M, (1 + k,), zm, t, j, tiles + 1)
                g = CQ[k, z - 2, ro, x]
                qn = q + rate * lq
                out[1 + k, z - 2, ro, x] = qn
                misfit = misfit + q * lq
                qterm = qterm + g * lq
                obj = obj + g * qn
            th = jnp.tanh(heat[r, x] - 0.5 * c)
            pq = p * (1.0 - p)
            drive = p - 0.5 + 0.6 * th
            dp = 0.08 * (lp + 4.0 * pq * drive + 0.2 * p * misfit)
            pn = p + dp
            cn = c + 0.064 * lc + 0.5 * dp * c
            out[0, z - 2, ro, x] = pn
            out[5, z - 2, ro, x] = cn
            obuf[...] += obj + g0 * pn + gc * cn
            w = 0.192 * pq * (1.0 - th * th)
            gw = gp * w
            lam_p = (
                gp * (1.0 + 0.08 * (4.0 * (1.0 - 2.0 * p) * drive + 4.0 * pq + 0.2 * misfit))
                + 0.08 * lgp
                - 0.5 * c * gc
                - 0.16 * (1.0 - p) * qterm
            )
            lam_c = gc * (1.0 + 0.5 * dp) + 0.064 * lgc - 0.5 * gw
            s = gw + (lam_p + 0.5 * E[5, z, r, x] * lam_c) * W0[zm, r, x]
            if edge is not None:
                s = s + W0[edge - 1, r, x] * (0.08 * gp + 0.032 * E[5, edge, r, x] * gc)
            b = (t - 1) * lanes + j
            sbuf[b] += s

    def grid(z0, zstep, t0, count, body):
        loop(2 * count, lambda i: body(z0 + zstep * (i // count), t0 + i % count))

    for copy in local[:3]:
        copy.wait()
    loop(D * tiles, lambda i: expand(2 + i // tiles, 1 + i % tiles))

    @pl.when(jnp.logical_not(is_low))
    def _():
        for copy in to_high:
            copy.wait_recv()
        loop(D, lambda i: expand(2 + i, 0))

    @pl.when(is_low)
    def _():
        loop(D + 2, lambda i: wipe(1 + i, 0))
        heat[pl.ds(0, 8), :] = jnp.zeros((8, cols), F32)
        for k in range(2):
            for z in range(D):
                G[k, 1 + z, pl.ds(0, 8), :] = jnp.zeros((8, cols), F32)

    @pl.when(jnp.logical_not(is_high))
    def _():
        for copy in to_low:
            copy.wait_recv()
        loop(D, lambda i: expand(2 + i, tiles + 1))

    @pl.when(is_high)
    def _():
        loop(D + 2, lambda i: wipe(1 + i, tiles + 1))
        heat[pl.ds(top, 8), :] = jnp.zeros((8, cols), F32)
        for k in range(2):
            for z in range(D):
                G[k, 1 + z, pl.ds(top, 8), :] = jnp.zeros((8, cols), F32)

    for copy in local[3:]:
        copy.wait()
    loop((D - 2) * (tiles + 2), lambda i: mid(3 + i // (tiles + 2), i % (tiles + 2), True))

    for copy in zc:
        copy.wait_recv()
    c_high, c_low = [], []
    i = 0
    for z in (1, D + 2):
        for _, dst in dests:
            c_high.append(
                remote(dst.at[z, pl.ds(rows, 8)], dst.at[z, pl.ds(0, 8)], csend.at[i], crecv.at[i], gz, high)
            )
            c_low.append(
                remote(dst.at[z, pl.ds(8, 8)], dst.at[z, pl.ds(top, 8)], csend.at[6 + i], crecv.at[6 + i], gz, low)
            )
            i += 1

    @pl.when(jnp.logical_not(is_high))
    def _():
        for copy in c_high:
            copy.start()

    @pl.when(jnp.logical_not(is_low))
    def _():
        for copy in c_low:
            copy.start()

    grid(1, D + 1, 1, tiles, expand)

    @pl.when(jnp.logical_not(is_low))
    def _():
        for copy in c_high:
            copy.wait_recv()
        loop(2, lambda i: expand(1 + (D + 1) * i, 0))

    @pl.when(jnp.logical_not(is_high))
    def _():
        for copy in c_low:
            copy.wait_recv()
        loop(2, lambda i: expand(1 + (D + 1) * i, tiles + 1))

    grid(2, D - 1, 0, tiles + 2, lambda z, t: mid(z, t, True))
    loop((D - 2) * tiles, lambda i: final(3 + i // tiles, 1 + i % tiles, None))

    def give(o):
        return remote(sbuf.at[pl.ds(o * per, per)], rbuf.at[gz], r1s.at[o], r1r.at[gz], o, gy)

    def take(o):
        return remote(sbuf.at[pl.ds(o * per, per)], rbuf.at[o], r1s.at[o], r1r.at[o], o, gy)

    def others(body):
        for o in range(n):

            @pl.when(gz != o)
            def _():
                body(o)

    given = 0
    for t in range(tiles):
        for copy in second(t):
            copy.wait_recv()

        def layers(i, t=t):
            z = 1 + (D + 1) * i
            expand(z - 1 + 2 * i, t + 1)
            mid(z, t + 1, False)
            final(2 + (D - 1) * i, t + 1, z)

        loop(2, layers)
        ready = n if t == tiles - 1 else (t + 1) * lanes // per
        for o in range(given, ready):

            @pl.when(gz != o)
            def _():
                give(o).start()

        given = ready

    sends = []
    for d in range(1, m):
        sends.append(remote(obuf, orbuf.at[gy], os.at[d - 1], orr.at[d - 1], gz, lax.rem(gy + d, m)))
    for copy in sends:
        copy.start()
    orbuf[gy] = obuf[...]
    rbuf[gz] = jnp.zeros((per, 8, 128), F32)
    for copy in sends:
        copy.wait_recv()
    others(lambda o: take(o).wait_recv())
    acc = sbuf[pl.ds(gz * per, per)]
    for d in range(n):
        acc = acc + rbuf[d]
    red[pl.ds(0, per)] = acc
    total = orbuf[0]
    for d in range(1, m):
        total = total + orbuf[d]
    red[per] = total
    bcast = []
    for d in range(1, n):
        bcast.append(remote(red, fin.at[gz], r2s.at[d - 1], r2r.at[d - 1], lax.rem(gz + d, n), gy))
    for copy in bcast:
        copy.start()
    fin[gz] = red[...]
    for copy in bcast:
        copy.wait_recv()
    total = fin[0, per]
    for d in range(1, n):
        total = total + fin[d, per]
    obj_out[0, 0] = jnp.sum(total)
    for b in range(tiles * lanes):
        sens_out[pl.ds(b // lanes * 8, 8), pl.ds(b % lanes * 128, 128)] = fin[b // per, b % per]

    for copy in zc + sends + bcast:
        copy.wait_send()
    others(lambda o: give(o).wait_send())
    for t in range(tiles):
        for copy in second(t):
            copy.wait_send()

    @pl.when(jnp.logical_not(is_high))
    def _():
        for copy in to_high + c_high:
            copy.wait_send()

    @pl.when(jnp.logical_not(is_low))
    def _():
        for copy in to_low + c_low:
            copy.wait_send()


def solution(mesh):
    n, m = mesh.shape["gz"], mesh.shape["gy"]

    def on_device(phase, solute, labels, quat_table, heat_map, cotangent):
        depth, rows, cols = phase.shape
        blocks = rows // 8 * (cols // 128)
        per = -(-blocks // n)
        tall = rows + 16
        vmem = pl.BlockSpec(memory_space=pltpu.VMEM)
        hbm = pl.BlockSpec(memory_space=pltpu.HBM)
        smem = pl.BlockSpec(memory_space=pltpu.SMEM)
        fine = pltpu.SemaphoreType.DMA((6, rows // 8))
        dma = lambda k: pltpu.SemaphoreType.DMA((k,))
        final, sens, obj = pl.pallas_call(
            functools.partial(kernel, n, m, depth, rows, cols, per),
            out_shape=(
                jax.ShapeDtypeStruct((6, depth, rows, cols), F32),
                jax.ShapeDtypeStruct((rows, cols), F32),
                jax.ShapeDtypeStruct((1, 1), F32),
            ),
            in_specs=[hbm, hbm, hbm, smem, hbm, hbm],
            out_specs=(vmem, vmem, smem),
            scratch_shapes=[
                pltpu.VMEM((6, depth + 4, tall, cols), F32),
                pltpu.VMEM((depth + 4, tall, cols), jnp.int32),
                pltpu.VMEM((6, depth + 2, tall, cols), F32),
                pltpu.VMEM((2, depth + 2, tall, cols), F32),
                pltpu.VMEM((depth + 2, tall, cols), F32),
                pltpu.VMEM((4, depth, rows, cols), F32),
                pltpu.VMEM((depth + 2, tall, cols), F32),
                pltpu.VMEM((tall, cols), F32),
                pltpu.VMEM((4, 8, 128), F32),
                pltpu.VMEM((n * per, 8, 128), F32),
                pltpu.VMEM((n, per, 8, 128), F32),
                pltpu.VMEM((8, 128), F32),
                pltpu.VMEM((m, 8, 128), F32),
                pltpu.VMEM((per + 1, 8, 128), F32),
                pltpu.VMEM((n, per + 1, 8, 128), F32),
                dma(7), dma(12), dma(12), dma(6), dma(6), fine, fine, dma(12), dma(12),
                dma(n), dma(n), dma(m - 1), dma(m - 1), dma(n - 1), dma(n - 1),
            ],
            compiler_params=pltpu.CompilerParams(
                collective_id=0, has_side_effects=True, vmem_limit_bytes=58 * 1024 * 1024
            ),
        )(phase, solute, labels, quat_table, heat_map, cotangent)
        return final, sens, obj[0, 0]

    return jax.shard_map(
        on_device,
        mesh=mesh,
        in_specs=(
            P("gz", "gy", None),
            P("gz", "gy", None),
            P("gz", "gy", None),
            P(),
            P("gy", None),
            P(None, "gz", "gy", None),
        ),
        out_specs=(P(None, "gz", "gy", None), P("gy", None), P()),
        check_vma=False,
    )
```

```python
import functools

import jax
import jax.numpy as jnp
from jax import lax
from jax.experimental import pallas as pl
from jax.experimental.pallas import tpu as pltpu
from jax.sharding import PartitionSpec as P

MESH = pl.DeviceIdType.MESH
F32 = jnp.float32


def kernel(
    n, m, depth, rows, cols, per,
    phase, solute, labels, quats, heat_in, cot,
    out, sens_out, obj_out,
    E, lab, M, G, GP, CQ, W0, heat, table, sbuf, rbuf, obuf, orbuf, red, fin,
    lsem, ysend, yrecv, zsend, zrecv, fsend, frecv, csend, crecv, r1s, r1r, os, orr, r2s, r2r,
):
    gz = lax.axis_index("gz")
    gy = lax.axis_index("gy")
    up = lax.rem(gz + 1, n)
    down = lax.rem(gz + n - 1, n)
    is_low = gy == 0
    is_high = gy == m - 1
    low = jnp.maximum(gy - 1, 0)
    high = jnp.minimum(gy + 1, m - 1)
    tiles = rows // 8
    lanes = cols // 128
    D = depth
    own = pl.ds(8, rows)
    top = 8 + rows

    bar = pltpu.get_barrier_semaphore()
    for d in range(1, n):
        pl.semaphore_signal(bar, inc=1, device_id=(lax.rem(gz + d, n), gy), device_id_type=MESH)
    for d in range(1, m):
        pl.semaphore_signal(bar, inc=1, device_id=(gz, lax.rem(gy + d, m)), device_id_type=MESH)

    local = []
    dests = ((phase, E.at[0]), (solute, E.at[5]), (labels, lab))
    for k, (src, dst) in enumerate(dests):
        local.append(pltpu.make_async_copy(src, dst.at[pl.ds(2, D), own], lsem.at[k]))
    local.append(pltpu.make_async_copy(cot.at[0], G.at[0, pl.ds(1, D), own], lsem.at[3]))
    local.append(pltpu.make_async_copy(cot.at[5], G.at[1, pl.ds(1, D), own], lsem.at[4]))
    local.append(pltpu.make_async_copy(cot.at[pl.ds(1, 4)], CQ, lsem.at[5]))
    local.append(pltpu.make_async_copy(heat_in, heat.at[own], lsem.at[6]))
    for copy in local:
        copy.start()

    pl.semaphore_wait(bar, n - 1 + m - 1)

    def remote(src, dst, ss, rs, z, y):
        return pltpu.make_async_remote_copy(
            src_ref=src, dst_ref=dst, send_sem=ss, recv_sem=rs, device_id=(z, y), device_id_type=MESH
        )

    zc = []
    for k, (src, dst) in enumerate(dests):
        zc.append(remote(src.at[D - 1], dst.at[1, own], zsend.at[2 * k], zrecv.at[2 * k], up, gy))
        zc.append(remote(src.at[0], dst.at[D + 2, own], zsend.at[2 * k + 1], zrecv.at[2 * k + 1], down, gy))

    def second(t):
        found = []
        a, b = pl.ds(pl.multiple_of(t * 8, 8), 8), pl.ds(pl.multiple_of(t * 8 + 8, 8), 8)
        for k, (src, dst) in enumerate(dests):
            found.append(remote(src.at[D - 2, a], dst.at[0, b], fsend.at[2 * k, t], frecv.at[2 * k, t], up, gy))
            found.append(
                remote(src.at[1, a], dst.at[D + 3, b], fsend.at[2 * k + 1, t], frecv.at[2 * k + 1, t], down, gy)
            )
        return found

    for copy in zc:
        copy.start()
    to_high, to_low = [], []
    faces = [(s, d.at[pl.ds(2, D)]) for s, d in dests]
    faces += [(cot.at[0], G.at[0, pl.ds(1, D)]), (cot.at[5], G.at[1, pl.ds(1, D)])]
    for k, (src, dst) in enumerate(faces):
        to_high.append(
            remote(src.at[:, pl.ds(rows - 8, 8)], dst.at[:, pl.ds(0, 8)], ysend.at[k], yrecv.at[k], gz, high)
        )
        to_low.append(
            remote(src.at[:, pl.ds(0, 8)], dst.at[:, pl.ds(top, 8)], ysend.at[6 + k], yrecv.at[6 + k], gz, low)
        )
    to_high.append(
        remote(heat_in.at[pl.ds(rows - 8, 8)], heat.at[pl.ds(0, 8)], ysend.at[5], yrecv.at[5], gz, high)
    )
    to_low.append(remote(heat_in.at[pl.ds(0, 8)], heat.at[pl.ds(top, 8)], ysend.at[11], yrecv.at[11], gz, low))

    @pl.when(jnp.logical_not(is_high))
    def _():
        for copy in to_high:
            copy.start()

    @pl.when(jnp.logical_not(is_low))
    def _():
        for copy in to_low:
            copy.start()

    for t in range(tiles):
        for copy in second(t):
            copy.start()

    row = lax.broadcasted_iota(jnp.int32, (8, 128), 0)
    lane = lax.broadcasted_iota(jnp.int32, (8, 128), 1)
    zero = jnp.zeros((8, 128), F32)

    for k in range(4):
        entry = zero
        for grain in range(quats.shape[1]):
            entry = jnp.where(lane == grain, quats[k, grain], entry)
        table[k] = entry
    sbuf[...] = jnp.zeros_like(sbuf)
    obuf[...] = jnp.zeros_like(obuf)
    for z in (0, D + 1):
        G[1, z] = jnp.zeros((rows + 16, cols), F32)
        GP[z] = jnp.zeros((rows + 16, cols), F32)

    def ds8(t):
        return pl.ds(pl.multiple_of(t * 8, 8), 8)

    def expand(z, t):
        r = ds8(t)
        for j in range(lanes):
            x = pl.ds(j * 128, 128)
            ids = lab[z, r, x]
            for k in range(4):
                E[1 + k, z, r, x] = jnp.take_along_axis(table[k], ids, axis=1)

    def wipe(z, t):
        r = ds8(t)
        for k in range(6):
            E[k, z, r, :] = jnp.zeros((8, cols), F32)

    def loop(count, body):
        def step(i, carry):
            body(i)
            return carry

        lax.fori_loop(0, count, step, 0)

    def around(ref, lead, z, t, j, last):
        r, x = ds8(t), pl.ds(j * 128, 128)
        c = ref[(*lead, z, r, x)]
        before = ref[(*lead, z, ds8(jnp.maximum(t - 1, 0)), x)]
        after = ref[(*lead, z, ds8(jnp.minimum(t + 1, last)), x)]
        left = ref[(*lead, z, r, pl.ds((j - 1) * 128, 128))] if j else zero
        right = ref[(*lead, z, r, pl.ds((j + 1) * 128, 128))] if j < lanes - 1 else zero
        ys = pltpu.roll(jnp.where(row == 0, after, c), 7, 0) + pltpu.roll(jnp.where(row == 7, before, c), 1, 0)
        xs = pltpu.roll(jnp.where(lane == 0, right, c), 127, 1) + pltpu.roll(jnp.where(lane == 127, left, c), 1, 1)
        zs = ref[(*lead, z + 1, r, x)] + ref[(*lead, z - 1, r, x)]
        return c, zs + ys + xs - 6.0 * c

    def mid(z, t, inside):
        r = ds8(t)
        drop = ((t == 0) & is_low) | ((t == tiles + 1) & is_high)
        keep = jnp.where(drop, 0.0, 1.0)
        hr = ds8(t)
        for j in range(lanes):
            x = pl.ds(j * 128, 128)
            p, lp = around(E, (0,), z, t, j, tiles + 1)
            c, lc = around(E, (5,), z, t, j, tiles + 1)
            misfit = zero
            rate = 0.08 * ((1.0 - p) * (1.0 - p) + 0.1)
            for k in range(4):
                q, lq = around(E, (1 + k,), z, t, j, tiles + 1)
                misfit = misfit + q * lq
                M[1 + k, z - 1, r, x] = keep * (q + rate * lq)
            th = jnp.tanh(heat[hr, x] - 0.5 * c)
            pq = p * (1.0 - p)
            dp = 0.08 * (lp + 4.0 * pq * (p - 0.5 + 0.6 * th) + 0.2 * p * misfit)
            cn = keep * (c + 0.064 * lc + 0.5 * dp * c)
            M[0, z - 1, r, x] = keep * (p + dp)
            M[5, z - 1, r, x] = cn
            W0[z - 1, r, x] = 0.192 * pq * (1.0 - th * th)
            if inside:
                GP[z - 1, r, x] = G[0, z - 1, r, x] + 0.5 * cn * G[1, z - 1, r, x]

    def final(z, t, edge):
        zm = z - 1
        r = ds8(t)
        ro = ds8(t - 1)
        for j in range(lanes):
            x = pl.ds(j * 128, 128)
            p, lp = around(M, (0,), zm, t, j, tiles + 1)
            c, lc = around(M, (5,), zm, t, j, tiles + 1)
            gc, lgc = around(G, (1,), zm, t, j, tiles + 1)
            gp, lgp = around(GP, (), zm, t, j, tiles + 1)
            g0 = G[0, zm, r, x]
            rate = 0.08 * ((1.0 - p) * (1.0 - p) + 0.1)
            misfit, qterm, obj = zero, zero, zero
            for k in range(4):
                q, lq = around(M, (1 + k,), zm, t, j, tiles + 1)
                g = CQ[k, z - 2, ro, x]
                qn = q + rate * lq
                out[1 + k, z - 2, ro, x] = qn
                misfit = misfit + q * lq
                qterm = qterm + g * lq
                obj = obj + g * qn
            th = jnp.tanh(heat[r, x] - 0.5 * c)
            pq = p * (1.0 - p)
            drive = p - 0.5 + 0.6 * th
            dp = 0.08 * (lp + 4.0 * pq * drive + 0.2 * p * misfit)
            pn = p + dp
            cn = c + 0.064 * lc + 0.5 * dp * c
            out[0, z - 2, ro, x] = pn
            out[5, z - 2, ro, x] = cn
            obuf[...] += obj + g0 * pn + gc * cn
            w = 0.192 * pq * (1.0 - th * th)
            gw = gp * w
            lam_p = (
                gp * (1.0 + 0.08 * (4.0 * (1.0 - 2.0 * p) * drive + 4.0 * pq + 0.2 * misfit))
                + 0.08 * lgp
                - 0.5 * c * gc
                - 0.16 * (1.0 - p) * qterm
            )
            lam_c = gc * (1.0 + 0.5 * dp) + 0.064 * lgc - 0.5 * gw
            s = gw + (lam_p + 0.5 * E[5, z, r, x] * lam_c) * W0[zm, r, x]
            if edge is not None:
                s = s + W0[edge - 1, r, x] * (0.08 * gp + 0.032 * E[5, edge, r, x] * gc)
            b = (t - 1) * lanes + j
            sbuf[b] += s

    def grid(z0, zstep, t0, count, body):
        loop(2 * count, lambda i: body(z0 + zstep * (i // count), t0 + i % count))

    for copy in local[:3]:
        copy.wait()
    loop(D * tiles, lambda i: expand(2 + i // tiles, 1 + i % tiles))

    @pl.when(jnp.logical_not(is_low))
    def _():
        for copy in to_high:
            copy.wait_recv()
        loop(D, lambda i: expand(2 + i, 0))

    @pl.when(is_low)
    def _():
        loop(D + 2, lambda i: wipe(1 + i, 0))
        heat[pl.ds(0, 8), :] = jnp.zeros((8, cols), F32)
        for k in range(2):
            for z in range(D):
                G[k, 1 + z, pl.ds(0, 8), :] = jnp.zeros((8, cols), F32)

    @pl.when(jnp.logical_not(is_high))
    def _():
        for copy in to_low:
            copy.wait_recv()
        loop(D, lambda i: expand(2 + i, tiles + 1))

    @pl.when(is_high)
    def _():
        loop(D + 2, lambda i: wipe(1 + i, tiles + 1))
        heat[pl.ds(top, 8), :] = jnp.zeros((8, cols), F32)
        for k in range(2):
            for z in range(D):
                G[k, 1 + z, pl.ds(top, 8), :] = jnp.zeros((8, cols), F32)

    for copy in local[3:]:
        copy.wait()
    loop((D - 2) * (tiles + 2), lambda i: mid(3 + i // (tiles + 2), i % (tiles + 2), True))

    for copy in zc:
        copy.wait_recv()
    c_high, c_low = [], []
    i = 0
    for z in (1, D + 2):
        for _, dst in dests:
            c_high.append(
                remote(dst.at[z, pl.ds(rows, 8)], dst.at[z, pl.ds(0, 8)], csend.at[i], crecv.at[i], gz, high)
            )
            c_low.append(
                remote(dst.at[z, pl.ds(8, 8)], dst.at[z, pl.ds(top, 8)], csend.at[6 + i], crecv.at[6 + i], gz, low)
            )
            i += 1

    @pl.when(jnp.logical_not(is_high))
    def _():
        for copy in c_high:
            copy.start()

    @pl.when(jnp.logical_not(is_low))
    def _():
        for copy in c_low:
            copy.start()

    grid(1, D + 1, 1, tiles, expand)

    @pl.when(jnp.logical_not(is_low))
    def _():
        for copy in c_high:
            copy.wait_recv()
        loop(2, lambda i: expand(1 + (D + 1) * i, 0))

    @pl.when(jnp.logical_not(is_high))
    def _():
        for copy in c_low:
            copy.wait_recv()
        loop(2, lambda i: expand(1 + (D + 1) * i, tiles + 1))

    grid(2, D - 1, 0, tiles + 2, lambda z, t: mid(z, t, True))
    loop((D - 2) * tiles, lambda i: final(3 + i // tiles, 1 + i % tiles, None))

    def give(o):
        return remote(sbuf.at[pl.ds(o * per, per)], rbuf.at[gz], r1s.at[o], r1r.at[gz], o, gy)

    def take(o):
        return remote(sbuf.at[pl.ds(o * per, per)], rbuf.at[o], r1s.at[o], r1r.at[o], o, gy)

    def others(body):
        for o in range(n):

            @pl.when(gz != o)
            def _():
                body(o)

    given = 0
    for t in range(tiles):
        for copy in second(t):
            copy.wait_recv()

        def layers(i, t=t):
            z = 1 + (D + 1) * i
            expand(z - 1 + 2 * i, t + 1)
            mid(z, t + 1, False)
            final(2 + (D - 1) * i, t + 1, z)

        loop(2, layers)
        ready = n if t == tiles - 1 else (t + 1) * lanes // per
        for o in range(given, ready):

            @pl.when(gz != o)
            def _():
                give(o).start()

        given = ready

    sends = []
    for d in range(1, m):
        sends.append(remote(obuf, orbuf.at[gy], os.at[d - 1], orr.at[d - 1], gz, lax.rem(gy + d, m)))
    for copy in sends:
        copy.start()
    orbuf[gy] = obuf[...]
    rbuf[gz] = jnp.zeros((per, 8, 128), F32)
    for copy in sends:
        copy.wait_recv()
    others(lambda o: take(o).wait_recv())
    acc = sbuf[pl.ds(gz * per, per)]
    for d in range(n):
        acc = acc + rbuf[d]
    red[pl.ds(0, per)] = acc
    total = orbuf[0]
    for d in range(1, m):
        total = total + orbuf[d]
    red[per] = total
    bcast = []
    for d in range(1, n):
        bcast.append(remote(red, fin.at[gz], r2s.at[d - 1], r2r.at[d - 1], lax.rem(gz + d, n), gy))
    for copy in bcast:
        copy.start()
    fin[gz] = red[...]
    for copy in bcast:
        copy.wait_recv()
    total = fin[0, per]
    for d in range(1, n):
        total = total + fin[d, per]
    obj_out[0, 0] = jnp.sum(total)
    for b in range(tiles * lanes):
        sens_out[pl.ds(b // lanes * 8, 8), pl.ds(b % lanes * 128, 128)] = fin[b // per, b % per]

    for copy in zc + sends + bcast:
        copy.wait_send()
    others(lambda o: give(o).wait_send())
    for t in range(tiles):
        for copy in second(t):
            copy.wait_send()

    @pl.when(jnp.logical_not(is_high))
    def _():
        for copy in to_high + c_high:
            copy.wait_send()

    @pl.when(jnp.logical_not(is_low))
    def _():
        for copy in to_low + c_low:
            copy.wait_send()


def solution(mesh):
    n, m = mesh.shape["gz"], mesh.shape["gy"]

    def on_device(phase, solute, labels, quat_table, heat_map, cotangent):
        depth, rows, cols = phase.shape
        blocks = rows // 8 * (cols // 128)
        per = -(-blocks // n)
        tall = rows + 16
        vmem = pl.BlockSpec(memory_space=pltpu.VMEM)
        hbm = pl.BlockSpec(memory_space=pltpu.HBM)
        smem = pl.BlockSpec(memory_space=pltpu.SMEM)
        fine = pltpu.SemaphoreType.DMA((6, rows // 8))
        dma = lambda k: pltpu.SemaphoreType.DMA((k,))
        final, sens, obj = pl.pallas_call(
            functools.partial(kernel, n, m, depth, rows, cols, per),
            out_shape=(
                jax.ShapeDtypeStruct((6, depth, rows, cols), F32),
                jax.ShapeDtypeStruct((rows, cols), F32),
                jax.ShapeDtypeStruct((1, 1), F32),
            ),
            in_specs=[hbm, hbm, hbm, smem, hbm, hbm],
            out_specs=(vmem, vmem, smem),
            scratch_shapes=[
                pltpu.VMEM((6, depth + 4, tall, cols), F32),
                pltpu.VMEM((depth + 4, tall, cols), jnp.int32),
                pltpu.VMEM((6, depth + 2, tall, cols), F32),
                pltpu.VMEM((2, depth + 2, tall, cols), F32),
                pltpu.VMEM((depth + 2, tall, cols), F32),
                pltpu.VMEM((4, depth, rows, cols), F32),
                pltpu.VMEM((depth + 2, tall, cols), F32),
                pltpu.VMEM((tall, cols), F32),
                pltpu.VMEM((4, 8, 128), F32),
                pltpu.VMEM((n * per, 8, 128), F32),
                pltpu.VMEM((n, per, 8, 128), F32),
                pltpu.VMEM((8, 128), F32),
                pltpu.VMEM((m, 8, 128), F32),
                pltpu.VMEM((per + 1, 8, 128), F32),
                pltpu.VMEM((n, per + 1, 8, 128), F32),
                dma(7), dma(12), dma(12), dma(6), dma(6), fine, fine, dma(12), dma(12),
                dma(n), dma(n), dma(m - 1), dma(m - 1), dma(n - 1), dma(n - 1),
            ],
            compiler_params=pltpu.CompilerParams(
                collective_id=0, has_side_effects=True, vmem_limit_bytes=58 * 1024 * 1024
            ),
        )(phase, solute, labels, quat_table.T, heat_map, cotangent)
        return final, sens, obj[0, 0]

    return jax.shard_map(
        on_device,
        mesh=mesh,
        in_specs=(
            P("gz", "gy", None),
            P("gz", "gy", None),
            P("gz", "gy", None),
            P(),
            P("gy", None),
            P(None, "gz", "gy", None),
        ),
        out_specs=(P(None, "gz", "gy", None), P("gy", None), P()),
        check_vma=False,
    )
```
